32 devices in a mesh: row: 8 (over y, x, core), col: 4 (over z).
Axes of the slice: x: 2, y: 2, z: 4, core: 2. Of those that a mesh axis runs over, the one named last changes fastest.
Arguments:
- phase: float32 [4096, 2048], P('row', 'col'), may hold values from -1 to 1
- tile_mask: int32 [16, 8], P('row', 'col'), may hold values 0 or 1
Outputs:
- updated: float32 [4096, 2048], P('row', 'col')
- section: float32 [4096, 2048], P('row', 'col')
The draws below stay inside these ranges and needn't reach their ends.
All inputs are finite; a program needn't handle non-finite values. No bound on the sum of `tile_mask` on one device may be relied on, other than what follows from the above.
Results may differ from the reference program's by a relative error of at most 0.0003.
Values sent between devices are 32-bit elements; how exact they have to be, the bound alone decides.
A program may use at most 64 MiB of HBM per device.

```python
import jax
import jax.numpy as jnp
from jax import lax

TILE = 256
KRYLOV = 3
MROWS = 16
MCOLS = 8
NX = 4096
NY = 2048


def touch_ends(result, own_key, low, largest):
    index_at = [jax.random.randint(jax.random.fold_in(own_key, axis), (), 0, length) for axis, length in enumerate(result.shape)]
    widest = result.shape.index(max(result.shape))
    beside = index_at[:widest] + [(index_at[widest] + 1) % result.shape[widest]] + index_at[widest + 1:]
    return result.at[tuple(index_at)].set(low).at[tuple(beside)].set(largest)


def steps_of(own_key, shape, split, low, high):
    def one(position, parts):
        steps = jax.random.uniform(jax.random.fold_in(jax.random.fold_in(own_key, 6), position), (parts,), jnp.float32, low / len(split), high / len(split))
        return jnp.repeat(jnp.exp(steps), shape[position] // parts).reshape((-1,) + (1,) * (len(shape) - position - 1))

    loudness = one(*split[0])
    for cut in split[1:]:
        loudness = loudness * one(*cut)
    return loudness


def setup_inputs(seed: int = 0) -> dict:
    key_list = jax.random.split(jax.random.key(seed), 3)
    return {
        "phase": jnp.clip(jax.random.uniform(key_list[0], (NX, NY), jnp.float32, -1.0, 1.0) * steps_of(key_list[0], (NX, NY), ((0, 8), (1, 4)), -0.4, 0.0), -1.0, 1.0),
        "tile_mask": touch_ends((jax.random.randint(key_list[1], (MROWS, MCOLS), 0, 4) < 3).astype(jnp.int32), jax.random.fold_in(key_list[1], 1), 0, 1),
    }


diffusion = 2.0
remainder_weight = 32.0

def laplace(field):
    padded = jnp.pad(field, 1)
    return padded[2:, 1:-1] + padded[:-2, 1:-1] + padded[1:-1, 2:] + padded[1:-1, :-2] - 4.0 * field

def operate(field, coef, active):
    return active * (diffusion * laplace(field) + coef * field)

def exponential(matrix):
    size = matrix.shape[0]
    eye = jnp.eye(size, dtype=jnp.float32)
    scaled = matrix * (1.0 / 1024.0)
    term = eye
    total = eye
    for degree in range(1, 11):
        term = jnp.dot(term, scaled, precision=lax.Precision.HIGHEST) / float(degree)
        total = total + term
    for squaring in range(10):
        total = jnp.dot(total, total, precision=lax.Precision.HIGHEST)
    return total

def phi_column(hess, scale, order):
    width = hess.shape[0]
    size = width + order
    augmented = jnp.zeros((size, size), jnp.float32)
    augmented = augmented.at[:width, :width].set(scale * hess)
    augmented = augmented.at[0, width].set(1.0)
    for offset in range(order - 1):
        augmented = augmented.at[width + offset, width + offset + 1].set(1.0)
    return exponential(augmented)[:width, size - 1]

def arnoldi(start, coef, active):
    beta = jnp.sqrt(jnp.sum(start * start))
    basis = [start / beta]
    hess = jnp.zeros((KRYLOV, KRYLOV), jnp.float32)
    for column in range(KRYLOV):
        image = operate(basis[column], coef, active)
        coeffs = jnp.stack([jnp.sum(vector * image) for vector in basis])
        hess = hess.at[:column + 1, column].set(coeffs)
        if column + 1 < KRYLOV:
            rest = image
            for index_k in range(column + 1):
                rest = rest - coeffs[index_k] * basis[index_k]
            length = jnp.sqrt(jnp.sum(rest * rest))
            hess = hess.at[column + 1, column].set(length)
            basis.append(rest / length)
    return (beta, basis, hess)

def combine(beta, basis, weights):
    total = jnp.zeros_like(basis[0])
    for index_k in range(len(basis)):
        total = total + weights[index_k] * basis[index_k]
    return beta * total

def reference(phase, tile_mask):
    masks = tile_mask.astype(jnp.float32)
    active = jnp.repeat(jnp.repeat(masks, TILE, axis=0), TILE, axis=1)
    force = operate(phase, 1.0 - phase * phase, active)
    slope = 1.0 - 3.0 * phase * phase
    beta_one, basis_one, hess_one = arnoldi(force, slope, active)
    shift = 0.5 * combine(beta_one, basis_one, phi_column(hess_one, 0.5, 1))
    section = phase + shift
    remainder = -active * shift * shift * (shift + 3.0 * phase)
    beta_two, basis_two, hess_two = arnoldi(remainder, slope, active)
    first = combine(beta_one, basis_one, phi_column(hess_one, 1.0, 1))
    third = combine(beta_two, basis_two, phi_column(hess_two, 1.0, 3))
    updated = phase + first + remainder_weight * third
    return (updated, section)
```

```python
import functools

import jax
import jax.numpy as jnp
from jax import lax
from jax.experimental import pallas as pl
from jax.experimental.pallas import tpu as pltpu
from jax.sharding import PartitionSpec as P

TILE = 256
HALO = 8
LANES = 128
CHUNK = 16
MOMENTS = 6
MESH = pl.DeviceIdType.MESH

diffusion = 2.0
remainder_weight = 32.0
offset = -4.0 * diffusion

STEPS = ((-1, 0), (1, 0), (0, -1), (0, 1), (-1, -1), (-1, 1), (1, -1), (1, 1))
OPPOSITE = (1, 0, 3, 2, 7, 6, 5, 4)


def phi_weights(diag, lower_sq, scale, order):
    s = scale * (1.0 / 1024.0)
    zero = jnp.zeros_like(s)
    one = jnp.ones_like(s)
    hess = [
        [diag[0] * s, lower_sq[0] * s, None],
        [s, diag[1] * s, lower_sq[1] * s],
        [None, s, diag[2] * s],
    ]
    eps = 1.0 / 1024.0
    term = [[one if i == j else zero for j in range(3)] for i in range(3)]
    total = [row[:] for row in term]
    side_term = [[zero] * order for _ in range(3)]
    side = [[zero] * order for _ in range(3)]
    tail = [1.0]
    for k in range(1, order):
        tail.append(tail[-1] * eps / k)
    for degree in range(1, 11):
        inv = 1.0 / degree
        new_term, new_side = [], []
        for i in range(3):
            row = []
            for j in range(3):
                acc = None
                for k in range(3):
                    if hess[k][j] is not None:
                        part = term[i][k] * hess[k][j]
                        acc = part if acc is None else acc + part
                row.append(acc * inv)
            new_term.append(row)
            new_side.append(
                [(term[i][0] if c == 0 else side_term[i][c - 1]) * (eps * inv) for c in range(order)]
            )
        term, side_term = new_term, new_side
        total = [[total[i][j] + term[i][j] for j in range(3)] for i in range(3)]
        side = [[side[i][c] + side_term[i][c] for c in range(order)] for i in range(3)]
    for _ in range(10):
        new_side = []
        for i in range(3):
            row = []
            for c in range(order):
                acc = side[i][c]
                for k in range(c):
                    acc = acc + side[i][k] * tail[c - k]
                for k in range(3):
                    acc = acc + total[i][k] * side[k][c]
                row.append(acc)
            new_side.append(row)
        total = [
            [
                total[i][0] * total[0][j] + total[i][1] * total[1][j] + total[i][2] * total[2][j]
                for j in range(3)
            ]
            for i in range(3)
        ]
        side = new_side
        tail = [sum(tail[k] * tail[c - k] for k in range(c + 1)) for c in range(order)]
    return [side[i][order - 1] for i in range(3)]


def lanczos(m):
    tiny = 1e-7
    a0 = m[1] / m[0]
    n1 = jnp.maximum(m[2] - a0 * m[1], tiny * m[2])
    h1 = n1 / m[0]
    a1 = (m[3] - 2.0 * a0 * m[2] + a0 * a0 * m[1]) / n1
    c1 = -(a0 + a1)
    c0 = a0 * a1 - h1
    n2 = jnp.maximum(m[4] + c1 * m[3] + c0 * m[2], tiny * m[4])
    h2 = n2 / n1
    a2 = (
        m[5] + 2.0 * c1 * m[4] + (c1 * c1 + 2.0 * c0) * m[3] + 2.0 * c0 * c1 * m[2] + c0 * c0 * m[1]
    ) / n2
    diag = [a0 + offset, a1 + offset, a2 + offset]
    return diag, [h1, h2], (a0, c1, c0)


def to_powers(y, coefs):
    a0, c1, c0 = coefs
    return (y[0] - a0 * y[1] + c0 * y[2], y[1] + c1 * y[2], y[2])


def kernel(
    n_row, n_col, phase_hbm, mask_ref, upd_hbm, sec_hbm,
    ph, a2, q, u0, u1, u2, w0, w1, w2, upd, sec,
    out_strip, in_side, in_corner, row_buf, gather,
    local_sem, side_send, side_recv, red_send, red_recv,
):
    rows, cols = upd.shape
    width = cols + LANES
    tall = rows + 2 * HALO
    n_dev = n_row * n_col
    my_row = lax.axis_index("row")
    my_col = lax.axis_index("col")
    me = my_row * n_col + my_col

    load = pltpu.make_async_copy(
        phase_hbm, ph.at[pl.ds(HALO, rows), pl.ds(0, cols)], local_sem.at[0]
    )
    load.start()

    barrier = pltpu.get_barrier_semaphore()

    def peer_of(d):
        peer = lax.rem(me + d, n_dev)
        return {"row": peer // n_col, "col": lax.rem(peer, n_col)}

    def greet(d, carry):
        pl.semaphore_signal(barrier, inc=1, device_id=peer_of(d), device_id_type=MESH)
        return carry

    lax.fori_loop(1, n_dev, greet, 0)

    def exists(k):
        dr, dc = STEPS[k]
        ok = None
        for cond in (
            my_row > 0 if dr < 0 else (my_row < n_row - 1 if dr > 0 else None),
            my_col > 0 if dc < 0 else (my_col < n_col - 1 if dc > 0 else None),
        ):
            if cond is not None:
                ok = cond if ok is None else jnp.logical_and(ok, cond)
        return ok

    def landing(k):
        return in_side.at[k] if k < 4 else in_corner.at[k - 4]

    def source(k):
        if k < 4:
            return out_strip.at[k]
        dr, dc = STEPS[k]
        return out_strip.at[0 if dr < 0 else 1, :, pl.ds(0 if dc < 0 else cols - LANES, LANES)]

    for k in range(8):
        @pl.when(jnp.logical_not(exists(k)))
        def _(k=k):
            if k < 4:
                in_side[k] = jnp.zeros((2 * HALO, cols), jnp.float32)
            else:
                in_corner[k - 4] = jnp.zeros((2 * HALO, LANES), jnp.float32)

    tile_rows, tile_cols = rows // TILE, cols // TILE
    value = [
        [mask_ref[i, j].astype(jnp.float32) * diffusion for j in range(tile_cols)]
        for i in range(tile_rows)
    ]
    for j in range(tile_cols):
        cut = pl.ds(j * TILE, TILE)
        out_strip[0, HALO:, cut] = jnp.full((HALO, TILE), value[0][j], jnp.float32)
        out_strip[1, HALO:, cut] = jnp.full((HALO, TILE), value[-1][j], jnp.float32)
        for i in range(tile_rows):
            a2[pl.ds(HALO + i * TILE, TILE), cut] = jnp.full((TILE, TILE), value[i][j], jnp.float32)
    for i in range(tile_rows):
        cut = pl.ds(i * TILE, TILE)
        out_strip[2, HALO:, cut] = jnp.full((HALO, TILE), value[i][0], jnp.float32)
        out_strip[3, HALO:, cut] = jnp.full((HALO, TILE), value[i][-1], jnp.float32)

    load.wait()
    out_strip[0, :HALO, :] = ph[pl.ds(HALO, HALO), pl.ds(0, cols)]
    out_strip[1, :HALO, :] = ph[pl.ds(rows, HALO), pl.ds(0, cols)]
    out_strip[2, :HALO, :] = ph[pl.ds(HALO, rows), pl.ds(0, LANES)].T[:HALO]
    out_strip[3, :HALO, :] = ph[pl.ds(HALO, rows), pl.ds(cols - LANES, LANES)].T[LANES - HALO:]

    pl.semaphore_wait(barrier, n_dev - 1)

    def side_copy(k):
        dr, dc = STEPS[k]
        return pltpu.make_async_remote_copy(
            src_ref=source(k),
            dst_ref=landing(OPPOSITE[k]),
            send_sem=side_send.at[k],
            recv_sem=side_recv.at[OPPOSITE[k]],
            device_id={"row": my_row + dr, "col": my_col + dc},
            device_id_type=MESH,
        )

    def side_arrival(k):
        dr, dc = STEPS[k]
        return pltpu.make_async_remote_copy(
            src_ref=landing(k),
            dst_ref=landing(k),
            send_sem=side_send.at[k],
            recv_sem=side_recv.at[k],
            device_id={"row": my_row + dr, "col": my_col + dc},
            device_id_type=MESH,
        )

    for k in range(8):
        @pl.when(exists(k))
        def _(k=k):
            side_copy(k).start()
    for k in range(8):
        @pl.when(exists(k))
        def _(k=k):
            side_arrival(k).wait_recv()

    lane = lax.broadcasted_iota(jnp.int32, (HALO, LANES), 1)
    halo_lanes = pl.ds(cols, LANES)
    gap = jnp.zeros((LANES - 2 * HALO, rows), jnp.float32)
    for part, ref in ((slice(0, HALO), ph), (slice(HALO, 2 * HALO), a2)):
        ref[pl.ds(0, HALO), pl.ds(0, cols)] = in_side[0, part, :]
        ref[pl.ds(HALO + rows, HALO), pl.ds(0, cols)] = in_side[1, part, :]
        ref[pl.ds(HALO, rows), halo_lanes] = jnp.concatenate(
            [in_side[3, part, :], gap, in_side[2, part, :]], axis=0
        ).T
        ref[pl.ds(0, HALO), halo_lanes] = jnp.where(
            lane < LANES // 2, in_corner[1, part, :], in_corner[0, part, :]
        )
        ref[pl.ds(HALO + rows, HALO), halo_lanes] = jnp.where(
            lane < LANES // 2, in_corner[3, part, :], in_corner[2, part, :]
        )

    def around(x, low, count):
        high = x.shape[0]
        centre = x[low:low + count]
        total = (
            pltpu.roll(x, 1, 0)[low:low + count]
            + pltpu.roll(x, high - 1, 0)[low:low + count]
            + pltpu.roll(centre, 1, 1)
            + pltpu.roll(centre, width - 1, 1)
        )
        return centre, total

    def fold(x):
        total = None
        for i in range(0, x.shape[0], 8):
            for j in range(0, cols, LANES):
                piece = x[i:i + 8, j:j + LANES]
                total = piece if total is None else total + piece
        return total

    def sweep(field, finish, n_sums, halo):
        if halo:
            finish(*around(field[pl.ds(0, 2 * HALO), :], 0, HALO), pl.ds(0, HALO))
            finish(
                *around(field[pl.ds(tall - 2 * HALO, 2 * HALO), :], HALO, HALO),
                pl.ds(tall - HALO, HALO),
            )

        def step(i, sums):
            start = pl.multiple_of(i * CHUNK, 8)
            x = field[pl.ds(start, CHUNK + 2 * HALO), :]
            terms = finish(
                *around(x, HALO, CHUNK), pl.ds(pl.multiple_of(start + HALO, 8), CHUNK)
            )
            return tuple(s + fold(t) for s, t in zip(sums, terms))

        zero = jnp.zeros((8, LANES), jnp.float32)
        return lax.fori_loop(0, rows // CHUNK, step, (zero,) * n_sums)

    def force_of(centre, near, at):
        act2 = a2[at, :]
        square = centre * centre
        act = act2 * (1.0 / diffusion)
        q[at, :] = act * (1.0 - 3.0 * square)
        u0[at, :] = act2 * (near - 4.0 * centre) + act * ((1.0 - square) * centre)
        return ()

    sweep(ph, force_of, 0, True)

    def power(dst, with_start):
        def finish(centre, near, at):
            image = a2[at, :] * near + q[at, :] * centre
            if dst is not None:
                dst[at, :] = image
            cross = centre * image
            if dst is None:
                return (cross,)
            if with_start:
                return (centre * centre, cross, image * image)
            return (cross, image * image)

        return finish

    def moments(b0, b1, b2, index):
        sums = sweep(b0, power(b1, True), 3, True)
        sums += sweep(b1, power(b2, False), 2, True)
        sums += sweep(b2, power(None, False), 1, False)
        lanes = lax.broadcasted_iota(jnp.int32, (1, LANES), 1)
        row = jnp.zeros((1, LANES), jnp.float32)
        for k, s in enumerate(sums):
            row = jnp.where(lanes == k, jnp.sum(s, keepdims=True), row)
        row_buf[index] = row
        gather[index, me] = row

        def send(d, carry):
            pltpu.make_async_remote_copy(
                src_ref=row_buf.at[index],
                dst_ref=gather.at[index, me],
                send_sem=red_send.at[index],
                recv_sem=red_recv.at[index],
                device_id=peer_of(d),
                device_id_type=MESH,
            ).start()
            return carry

        lax.fori_loop(1, n_dev, send, 0)
        others = gather.at[index, pl.ds(0, n_dev - 1)]
        done = pltpu.make_async_remote_copy(
            src_ref=others,
            dst_ref=others,
            send_sem=red_send.at[index],
            recv_sem=red_recv.at[index],
            device_id=peer_of(1),
            device_id_type=MESH,
        )
        done.wait_recv()
        done.wait_send()
        total = jnp.sum(gather[index], axis=0)
        total = jnp.broadcast_to(total, (8, LANES))
        spot = lax.broadcasted_iota(jnp.int32, (8, LANES), 1)
        return [
            jnp.broadcast_to(
                jnp.sum(jnp.where(spot == k, total, 0.0), axis=1, keepdims=True), (8, LANES)
            )
            for k in range(MOMENTS)
        ]

    def spread(x, count, wide):
        return jnp.broadcast_to(x, (count, wide))

    diag, lower, coefs = lanczos(moments(u0, u1, u2, 0))
    sub = lax.broadcasted_iota(jnp.int32, (8, LANES), 0)
    scale = jnp.where(sub < 4, 0.5, 1.0).astype(jnp.float32)
    mixed = to_powers(phi_weights(diag, lower, scale, 1), coefs)
    half = [0.5 * m[0:1, 0:1] for m in mixed]
    full = [m[4:5, 0:1] for m in mixed]

    def section_of(at, out_at):
        x0, x1, x2 = u0[at, :], u1[at, :], u2[at, :]
        here = ph[at, :]
        shift = half[0] * x0 + half[1] * x1 + half[2] * x2
        w0[at, :] = (a2[at, :] * (-1.0 / diffusion)) * shift * shift * (shift + 3.0 * here)
        if out_at is not None:
            sec[out_at, :] = (here + shift)[:, :cols]
            upd[out_at, :] = (here + full[0] * x0 + full[1] * x1 + full[2] * x2)[:, :cols]

    section_of(pl.ds(0, HALO), None)
    section_of(pl.ds(tall - HALO, HALO), None)

    def section_step(i, carry):
        start = pl.multiple_of(i * CHUNK, 8)
        section_of(pl.ds(pl.multiple_of(start + HALO, 8), CHUNK), pl.ds(start, CHUNK))
        return carry

    lax.fori_loop(0, rows // CHUNK, section_step, 0)
    put_sec = pltpu.make_async_copy(sec, sec_hbm, local_sem.at[1])
    put_sec.start()

    diag, lower, coefs = lanczos(moments(w0, w1, w2, 1))
    third = [
        remainder_weight * m[0:1, 0:1]
        for m in to_powers(phi_weights(diag, lower, jnp.ones((8, LANES), jnp.float32), 3), coefs)
    ]

    def final_step(i, carry):
        start = pl.multiple_of(i * CHUNK, 8)
        at = pl.ds(pl.multiple_of(start + HALO, 8), CHUNK)
        cut = pl.ds(0, cols)
        out_at = pl.ds(start, CHUNK)
        upd[out_at, :] = upd[out_at, :] + (
            third[0] * w0[at, cut] + third[1] * w1[at, cut] + third[2] * w2[at, cut]
        )
        return carry

    lax.fori_loop(0, rows // CHUNK, final_step, 0)
    put_upd = pltpu.make_async_copy(upd, upd_hbm, local_sem.at[2])
    put_upd.start()
    for k in range(8):
        @pl.when(exists(k))
        def _(k=k):
            side_copy(k).wait_send()
    put_sec.wait()
    put_upd.wait()


def body(n_row, n_col, phase, tile_mask):
    rows, cols = phase.shape
    n_dev = n_row * n_col
    block = pltpu.VMEM((rows + 2 * HALO, cols + LANES), jnp.float32)
    flat = pltpu.VMEM((rows, cols), jnp.float32)
    shape = jax.ShapeDtypeStruct((rows, cols), jnp.float32)
    hbm = pl.BlockSpec(memory_space=pl.ANY)
    return pl.pallas_call(
        functools.partial(kernel, n_row, n_col),
        out_shape=(shape, shape),
        in_specs=[hbm, pl.BlockSpec(memory_space=pltpu.SMEM)],
        out_specs=(hbm, hbm),
        scratch_shapes=[block] * 9 + [flat] * 2 + [
            pltpu.VMEM((4, 2 * HALO, cols), jnp.float32),
            pltpu.VMEM((4, 2 * HALO, cols), jnp.float32),
            pltpu.VMEM((4, 2 * HALO, LANES), jnp.float32),
            pltpu.VMEM((2, 1, LANES), jnp.float32),
            pltpu.VMEM((2, n_dev, 1, LANES), jnp.float32),
            pltpu.SemaphoreType.DMA((3,)),
            pltpu.SemaphoreType.DMA((8,)),
            pltpu.SemaphoreType.DMA((8,)),
            pltpu.SemaphoreType.DMA((2,)),
            pltpu.SemaphoreType.DMA((2,)),
        ],
        compiler_params=pltpu.CompilerParams(collective_id=0, has_side_effects=True),
        name="epirk_section",
    )(phase, tile_mask)


def solution(mesh):
    spec = P("row", "col")
    run = functools.partial(body, mesh.shape["row"], mesh.shape["col"])
    return jax.shard_map(
        run, mesh=mesh, in_specs=(spec, spec), out_specs=(spec, spec), check_vma=False
    )
```

```python
import functools

import jax
import jax.numpy as jnp
from jax import lax
from jax.experimental import pallas as pl
from jax.experimental.pallas import tpu as pltpu
from jax.sharding import PartitionSpec as P

TILE = 256
HALO = 8
LANES = 128
CHUNK = 64
FINAL = 64
MOMENTS = 6
MESH = pl.DeviceIdType.MESH

diffusion = 2.0
remainder_weight = 32.0
offset = -4.0 * diffusion

STEPS = ((-1, 0), (1, 0), (0, -1), (0, 1), (-1, -1), (-1, 1), (1, -1), (1, 1))
OPPOSITE = (1, 0, 3, 2, 7, 6, 5, 4)


def phi_weights(diag, lower_sq, scale, order):
    s = scale * (1.0 / 1024.0)
    zero = jnp.zeros_like(s)
    one = jnp.ones_like(s)
    hess = [
        [diag[0] * s, lower_sq[0] * s, None],
        [s, diag[1] * s, lower_sq[1] * s],
        [None, s, diag[2] * s],
    ]
    eps = 1.0 / 1024.0
    term = [[one if i == j else zero for j in range(3)] for i in range(3)]
    total = [row[:] for row in term]
    side_term = [[zero] * order for _ in range(3)]
    side = [[zero] * order for _ in range(3)]
    tail = [1.0]
    for k in range(1, order):
        tail.append(tail[-1] * eps / k)
    for degree in range(1, 11):
        inv = 1.0 / degree
        new_term, new_side = [], []
        for i in range(3):
            row = []
            for j in range(3):
                acc = None
                for k in range(3):
                    if hess[k][j] is not None:
                        part = term[i][k] * hess[k][j]
                        acc = part if acc is None else acc + part
                row.append(acc * inv)
            new_term.append(row)
            new_side.append(
                [(term[i][0] if c == 0 else side_term[i][c - 1]) * (eps * inv) for c in range(order)]
            )
        term, side_term = new_term, new_side
        total = [[total[i][j] + term[i][j] for j in range(3)] for i in range(3)]
        side = [[side[i][c] + side_term[i][c] for c in range(order)] for i in range(3)]
    for _ in range(10):
        new_side = []
        for i in range(3):
            row = []
            for c in range(order):
                acc = side[i][c]
                for k in range(c):
                    acc = acc + side[i][k] * tail[c - k]
                for k in range(3):
                    acc = acc + total[i][k] * side[k][c]
                row.append(acc)
            new_side.append(row)
        total = [
            [
                total[i][0] * total[0][j] + total[i][1] * total[1][j] + total[i][2] * total[2][j]
                for j in range(3)
            ]
            for i in range(3)
        ]
        side = new_side
        tail = [sum(tail[k] * tail[c - k] for k in range(c + 1)) for c in range(order)]
    return [side[i][order - 1] for i in range(3)]


def lanczos(m):
    tiny = 1e-7
    a0 = m[1] / m[0]
    n1 = jnp.maximum(m[2] - a0 * m[1], tiny * m[2])
    h1 = n1 / m[0]
    a1 = (m[3] - 2.0 * a0 * m[2] + a0 * a0 * m[1]) / n1
    c1 = -(a0 + a1)
    c0 = a0 * a1 - h1
    n2 = jnp.maximum(m[4] + c1 * m[3] + c0 * m[2], tiny * m[4])
    h2 = n2 / n1
    a2 = (
        m[5] + 2.0 * c1 * m[4] + (c1 * c1 + 2.0 * c0) * m[3] + 2.0 * c0 * c1 * m[2] + c0 * c0 * m[1]
    ) / n2
    diag = [a0 + offset, a1 + offset, a2 + offset]
    return diag, [h1, h2], (a0, c1, c0)


def to_powers(y, coefs):
    a0, c1, c0 = coefs
    return (y[0] - a0 * y[1] + c0 * y[2], y[1] + c1 * y[2], y[2])


def kernel(
    n_row, n_col, phase_hbm, mask_ref, upd_hbm, sec_hbm,
    ph, a2, q, u0, u1, u2, w0, w1, w2, upd, sec,
    out_strip, in_side, in_corner, row_buf, gather,
    local_sem, side_send, side_recv, red_send, red_recv,
):
    blocks, rows, _ = upd.shape
    cols = blocks * LANES
    tall = rows + 2 * HALO
    n_dev = n_row * n_col
    my_row = lax.axis_index("row")
    my_col = lax.axis_index("col")
    me = my_row * n_col + my_col

    def load(j):
        return pltpu.make_async_copy(
            phase_hbm.at[:, pl.ds(j * LANES, LANES)],
            ph.at[j, pl.ds(HALO, rows)],
            local_sem.at[j],
        )

    def put(j, src, dst, base):
        return pltpu.make_async_copy(
            src.at[j], dst.at[:, pl.ds(j * LANES, LANES)], local_sem.at[base + j]
        )

    for j in range(blocks):
        load(j).start()

    barrier = pltpu.get_barrier_semaphore()

    def peer_of(d):
        peer = lax.rem(me + d, n_dev)
        return {"row": peer // n_col, "col": lax.rem(peer, n_col)}

    def greet(d, carry):
        pl.semaphore_signal(barrier, inc=1, device_id=peer_of(d), device_id_type=MESH)
        return carry

    lax.fori_loop(1, n_dev, greet, 0)

    def exists(k):
        dr, dc = STEPS[k]
        ok = None
        for cond in (
            my_row > 0 if dr < 0 else (my_row < n_row - 1 if dr > 0 else None),
            my_col > 0 if dc < 0 else (my_col < n_col - 1 if dc > 0 else None),
        ):
            if cond is not None:
                ok = cond if ok is None else jnp.logical_and(ok, cond)
        return ok

    def landing(k):
        return in_side.at[k] if k < 4 else in_corner.at[k - 4]

    def source(k):
        if k < 4:
            return out_strip.at[k]
        dr, dc = STEPS[k]
        return out_strip.at[0 if dr < 0 else 1, :, pl.ds(0 if dc < 0 else cols - LANES, LANES)]

    for k in range(8):
        @pl.when(jnp.logical_not(exists(k)))
        def _(k=k):
            if k < 4:
                in_side[k] = jnp.zeros((2 * HALO, cols), jnp.float32)
            else:
                in_corner[k - 4] = jnp.zeros((2 * HALO, LANES), jnp.float32)

    tile_rows, tile_cols = rows // TILE, cols // TILE
    value = [
        [mask_ref[i, j].astype(jnp.float32) * diffusion for j in range(tile_cols)]
        for i in range(tile_rows)
    ]
    for j in range(tile_cols):
        cut = pl.ds(j * TILE, TILE)
        out_strip[0, HALO:, cut] = jnp.full((HALO, TILE), value[0][j], jnp.float32)
        out_strip[1, HALO:, cut] = jnp.full((HALO, TILE), value[-1][j], jnp.float32)
    for j in range(blocks):
        for i in range(tile_rows):
            a2[j, pl.ds(HALO + i * TILE, TILE), :] = jnp.full(
                (TILE, LANES), value[i][j * LANES // TILE], jnp.float32
            )
    for i in range(tile_rows):
        cut = pl.ds(i * TILE, TILE)
        out_strip[2, HALO:, cut] = jnp.full((HALO, TILE), value[i][0], jnp.float32)
        out_strip[3, HALO:, cut] = jnp.full((HALO, TILE), value[i][-1], jnp.float32)

    for j in range(blocks):
        load(j).wait()
    for j in range(blocks):
        cut = pl.ds(j * LANES, LANES)
        out_strip[0, :HALO, cut] = ph[j, pl.ds(HALO, HALO), :]
        out_strip[1, :HALO, cut] = ph[j, pl.ds(rows, HALO), :]
    out_strip[2, :HALO, :] = ph[0, pl.ds(HALO, rows), :].T[:HALO]
    out_strip[3, :HALO, :] = ph[blocks - 1, pl.ds(HALO, rows), :].T[LANES - HALO:]

    pl.semaphore_wait(barrier, n_dev - 1)

    def side_copy(k):
        dr, dc = STEPS[k]
        return pltpu.make_async_remote_copy(
            src_ref=source(k),
            dst_ref=landing(OPPOSITE[k]),
            send_sem=side_send.at[k],
            recv_sem=side_recv.at[OPPOSITE[k]],
            device_id={"row": my_row + dr, "col": my_col + dc},
            device_id_type=MESH,
        )

    def side_arrival(k):
        dr, dc = STEPS[k]
        return pltpu.make_async_remote_copy(
            src_ref=landing(k),
            dst_ref=landing(k),
            send_sem=side_send.at[k],
            recv_sem=side_recv.at[k],
            device_id={"row": my_row + dr, "col": my_col + dc},
            device_id_type=MESH,
        )

    for k in range(8):
        @pl.when(exists(k))
        def _(k=k):
            side_copy(k).start()
    for k in range(8):
        @pl.when(exists(k))
        def _(k=k):
            side_arrival(k).wait_recv()

    lane = lax.broadcasted_iota(jnp.int32, (HALO, LANES), 1)
    gap = jnp.zeros((LANES - 2 * HALO, rows), jnp.float32)
    for part, ref in ((slice(0, HALO), ph), (slice(HALO, 2 * HALO), a2)):
        for j in range(blocks):
            cut = pl.ds(j * LANES, LANES)
            ref[j, pl.ds(0, HALO), :] = in_side[0, part, cut]
            ref[j, pl.ds(HALO + rows, HALO), :] = in_side[1, part, cut]
        ref[blocks, pl.ds(HALO, rows), :] = jnp.concatenate(
            [in_side[3, part, :], gap, in_side[2, part, :]], axis=0
        ).T
        ref[blocks, pl.ds(0, HALO), :] = jnp.where(
            lane < LANES // 2, in_corner[1, part, :], in_corner[0, part, :]
        )
        ref[blocks, pl.ds(HALO + rows, HALO), :] = jnp.where(
            lane < LANES // 2, in_corner[3, part, :], in_corner[2, part, :]
        )

    def around(field, at, above, below, count, outer):
        column = lax.broadcasted_iota(jnp.int32, (count, LANES), 1)
        centre = [field[j, at, :] for j in range(blocks + 1)]
        ahead = [pltpu.roll(x, 1, 1) for x in centre]
        behind = [pltpu.roll(x, LANES - 1, 1) for x in centre]
        n = blocks + 1
        for j in range(n if outer else blocks):
            near = (
                field[j, above, :]
                + field[j, below, :]
                + jnp.where(column == 0, ahead[(j - 1) % n], ahead[j])
                + jnp.where(column == LANES - 1, behind[(j + 1) % n], behind[j])
            )
            yield j, centre[j], near

    def sweep(field, finish, n_sums, halo):
        if halo:
            for first in (1, tall - 1 - HALO):
                at, above, below = (pl.ds(first + shift, HALO) for shift in (0, -1, 1))
                for j, centre, near in around(field, at, above, below, HALO, True):
                    finish(j, centre, near, at)

        def step(i, sums):
            start = pl.multiple_of(i * CHUNK, 8)
            at = pl.ds(pl.multiple_of(start + HALO, 8), CHUNK)
            above = pl.ds(start + (HALO - 1), CHUNK)
            below = pl.ds(start + (HALO + 1), CHUNK)
            for j, centre, near in around(field, at, above, below, CHUNK, halo):
                terms = finish(j, centre, near, at)
                if j < blocks:
                    sums = tuple(s + t for s, t in zip(sums, terms))
            return sums

        zero = jnp.zeros((CHUNK, LANES), jnp.float32)
        return lax.fori_loop(0, rows // CHUNK, step, (zero,) * n_sums)

    def force_of(j, centre, near, at):
        act2 = a2[j, at, :]
        square = centre * centre
        act = act2 * (1.0 / diffusion)
        q[j, at, :] = act * (1.0 - 3.0 * square)
        u0[j, at, :] = act2 * (near - 4.0 * centre) + act * ((1.0 - square) * centre)
        return ()

    sweep(ph, force_of, 0, True)

    def power(dst, with_start):
        def finish(j, centre, near, at):
            image = a2[j, at, :] * near + q[j, at, :] * centre
            if dst is not None:
                dst[j, at, :] = image
            cross = centre * image
            if dst is None:
                return (cross,)
            if with_start:
                return (centre * centre, cross, image * image)
            return (cross, image * image)

        return finish

    def moments(b0, b1, b2, index):
        sums = sweep(b0, power(b1, True), 3, True)
        sums += sweep(b1, power(b2, False), 2, True)
        sums += sweep(b2, power(None, False), 1, False)
        lanes = lax.broadcasted_iota(jnp.int32, (1, LANES), 1)
        row = jnp.zeros((1, LANES), jnp.float32)
        for k, s in enumerate(sums):
            row = jnp.where(lanes == k, jnp.sum(s, keepdims=True), row)
        row_buf[index] = row
        gather[index, me] = row

        def send(d, carry):
            pltpu.make_async_remote_copy(
                src_ref=row_buf.at[index],
                dst_ref=gather.at[index, me],
                send_sem=red_send.at[index],
                recv_sem=red_recv.at[index],
                device_id=peer_of(d),
                device_id_type=MESH,
            ).start()
            return carry

        lax.fori_loop(1, n_dev, send, 0)
        others = gather.at[index, pl.ds(0, n_dev - 1)]
        done = pltpu.make_async_remote_copy(
            src_ref=others,
            dst_ref=others,
            send_sem=red_send.at[index],
            recv_sem=red_recv.at[index],
            device_id=peer_of(1),
            device_id_type=MESH,
        )
        done.wait_recv()
        done.wait_send()
        total = jnp.sum(gather[index], axis=0)
        total = jnp.broadcast_to(total, (8, LANES))
        spot = lax.broadcasted_iota(jnp.int32, (8, LANES), 1)
        return [
            jnp.broadcast_to(
                jnp.sum(jnp.where(spot == k, total, 0.0), axis=1, keepdims=True), (8, LANES)
            )
            for k in range(MOMENTS)
        ]

    diag, lower, coefs = lanczos(moments(u0, u1, u2, 0))
    sub = lax.broadcasted_iota(jnp.int32, (8, LANES), 0)
    scale = jnp.where(sub < 4, 0.5, 1.0).astype(jnp.float32)
    mixed = to_powers(phi_weights(diag, lower, scale, 1), coefs)
    half = [0.5 * m[0:1, 0:1] for m in mixed]
    full = [m[4:5, 0:1] for m in mixed]

    def section_of(at, out_at):
        for j in range(blocks + 1):
            x0, x1, x2 = u0[j, at, :], u1[j, at, :], u2[j, at, :]
            here = ph[j, at, :]
            shift = half[0] * x0 + half[1] * x1 + half[2] * x2
            w0[j, at, :] = (a2[j, at, :] * (-1.0 / diffusion)) * shift * shift * (shift + 3.0 * here)
            if out_at is not None and j < blocks:
                sec[j, out_at, :] = here + shift
                upd[j, out_at, :] = here + full[0] * x0 + full[1] * x1 + full[2] * x2

    section_of(pl.ds(0, HALO), None)
    section_of(pl.ds(tall - HALO, HALO), None)

    def section_step(i, carry):
        start = pl.multiple_of(i * CHUNK, 8)
        section_of(pl.ds(pl.multiple_of(start + HALO, 8), CHUNK), pl.ds(start, CHUNK))
        return carry

    lax.fori_loop(0, rows // CHUNK, section_step, 0)
    for j in range(blocks):
        put(j, sec, sec_hbm, blocks).start()

    diag, lower, coefs = lanczos(moments(w0, w1, w2, 1))
    third = [
        remainder_weight * m[0:1, 0:1]
        for m in to_powers(phi_weights(diag, lower, jnp.ones((8, LANES), jnp.float32), 3), coefs)
    ]

    for j in range(blocks):
        def final_step(i, carry, j=j):
            start = pl.multiple_of(i * FINAL, 8)
            at = pl.ds(pl.multiple_of(start + HALO, 8), FINAL)
            out_at = pl.ds(start, FINAL)
            upd[j, out_at, :] = upd[j, out_at, :] + (
                third[0] * w0[j, at, :] + third[1] * w1[j, at, :] + third[2] * w2[j, at, :]
            )
            return carry

        lax.fori_loop(0, rows // FINAL, final_step, 0)
        put(j, upd, upd_hbm, 2 * blocks).start()
    for k in range(8):
        @pl.when(exists(k))
        def _(k=k):
            side_copy(k).wait_send()
    for j in range(blocks):
        put(j, sec, sec_hbm, blocks).wait()
        put(j, upd, upd_hbm, 2 * blocks).wait()


def body(n_row, n_col, phase, tile_mask):
    rows, cols = phase.shape
    n_dev = n_row * n_col
    blocks = cols // LANES
    block = pltpu.VMEM((blocks + 1, rows + 2 * HALO, LANES), jnp.float32)
    flat = pltpu.VMEM((blocks, rows, LANES), jnp.float32)
    shape = jax.ShapeDtypeStruct((rows, cols), jnp.float32)
    hbm = pl.BlockSpec(memory_space=pl.ANY)
    return pl.pallas_call(
        functools.partial(kernel, n_row, n_col),
        out_shape=(shape, shape),
        in_specs=[hbm, pl.BlockSpec(memory_space=pltpu.SMEM)],
        out_specs=(hbm, hbm),
        scratch_shapes=[block] * 9 + [flat] * 2 + [
            pltpu.VMEM((4, 2 * HALO, cols), jnp.float32),
            pltpu.VMEM((4, 2 * HALO, cols), jnp.float32),
            pltpu.VMEM((4, 2 * HALO, LANES), jnp.float32),
            pltpu.VMEM((2, 1, LANES), jnp.float32),
            pltpu.VMEM((2, n_dev, 1, LANES), jnp.float32),
            pltpu.SemaphoreType.DMA((3 * blocks,)),
            pltpu.SemaphoreType.DMA((8,)),
            pltpu.SemaphoreType.DMA((8,)),
            pltpu.SemaphoreType.DMA((2,)),
            pltpu.SemaphoreType.DMA((2,)),
        ],
        compiler_params=pltpu.CompilerParams(collective_id=0, has_side_effects=True),
        name="epirk_section",
    )(phase, tile_mask)


def solution(mesh):
    spec = P("row", "col")
    run = functools.partial(body, mesh.shape["row"], mesh.shape["col"])
    return jax.shard_map(
        run, mesh=mesh, in_specs=(spec, spec), out_specs=(spec, spec), check_vma=False
    )
```

```python
import functools

import jax
import jax.numpy as jnp
from jax import lax
from jax.experimental import pallas as pl
from jax.experimental.pallas import tpu as pltpu
from jax.sharding import PartitionSpec as P

TILE = 256
HALO = 8
LANES = 128
CHUNK = 128
FINAL = 64
MOMENTS = 6
MESH = pl.DeviceIdType.MESH

diffusion = 2.0
remainder_weight = 32.0
offset = -4.0 * diffusion

STEPS = ((-1, 0), (1, 0), (0, -1), (0, 1), (-1, -1), (-1, 1), (1, -1), (1, 1))
OPPOSITE = (1, 0, 3, 2, 7, 6, 5, 4)


def phi_weights(diag, lower_sq, scale, order):
    s = scale * (1.0 / 1024.0)
    zero = jnp.zeros_like(s)
    one = jnp.ones_like(s)
    hess = [
        [diag[0] * s, lower_sq[0] * s, None],
        [s, diag[1] * s, lower_sq[1] * s],
        [None, s, diag[2] * s],
    ]
    eps = 1.0 / 1024.0
    term = [[one if i == j else zero for j in range(3)] for i in range(3)]
    total = [row[:] for row in term]
    side_term = [[zero] * order for _ in range(3)]
    side = [[zero] * order for _ in range(3)]
    tail = [1.0]
    for k in range(1, order):
        tail.append(tail[-1] * eps / k)
    for degree in range(1, 11):
        inv = 1.0 / degree
        new_term, new_side = [], []
        for i in range(3):
            row = []
            for j in range(3):
                acc = None
                for k in range(3):
                    if hess[k][j] is not None:
                        part = term[i][k] * hess[k][j]
                        acc = part if acc is None else acc + part
                row.append(acc * inv)
            new_term.append(row)
            new_side.append(
                [(term[i][0] if c == 0 else side_term[i][c - 1]) * (eps * inv) for c in range(order)]
            )
        term, side_term = new_term, new_side
        total = [[total[i][j] + term[i][j] for j in range(3)] for i in range(3)]
        side = [[side[i][c] + side_term[i][c] for c in range(order)] for i in range(3)]
    for _ in range(10):
        new_side = []
        for i in range(3):
            row = []
            for c in range(order):
                acc = side[i][c]
                for k in range(c):
                    acc = acc + side[i][k] * tail[c - k]
                for k in range(3):
                    acc = acc + total[i][k] * side[k][c]
                row.append(acc)
            new_side.append(row)
        total = [
            [
                total[i][0] * total[0][j] + total[i][1] * total[1][j] + total[i][2] * total[2][j]
                for j in range(3)
            ]
            for i in range(3)
        ]
        side = new_side
        tail = [sum(tail[k] * tail[c - k] for k in range(c + 1)) for c in range(order)]
    return [side[i][order - 1] for i in range(3)]


def lanczos(m):
    tiny = 1e-7
    a0 = m[1] / m[0]
    n1 = jnp.maximum(m[2] - a0 * m[1], tiny * m[2])
    h1 = n1 / m[0]
    a1 = (m[3] - 2.0 * a0 * m[2] + a0 * a0 * m[1]) / n1
    c1 = -(a0 + a1)
    c0 = a0 * a1 - h1
    n2 = jnp.maximum(m[4] + c1 * m[3] + c0 * m[2], tiny * m[4])
    h2 = n2 / n1
    a2 = (
        m[5] + 2.0 * c1 * m[4] + (c1 * c1 + 2.0 * c0) * m[3] + 2.0 * c0 * c1 * m[2] + c0 * c0 * m[1]
    ) / n2
    diag = [a0 + offset, a1 + offset, a2 + offset]
    return diag, [h1, h2], (a0, c1, c0)


def to_powers(y, coefs):
    a0, c1, c0 = coefs
    return (y[0] - a0 * y[1] + c0 * y[2], y[1] + c1 * y[2], y[2])


def kernel(
    n_row, n_col, phase_hbm, mask_hbm, upd, sec,
    ph, a2, q, u0, u1, u2, w0, w1, w2, mask_ref,
    out_strip, in_side, in_corner, row_buf, gather,
    local_sem, side_send, side_recv, red_send, red_recv,
):
    rows, cols = upd.shape
    blocks = cols // LANES
    tall = rows + 2 * HALO
    n_dev = n_row * n_col
    my_row = lax.axis_index("row")
    my_col = lax.axis_index("col")
    me = my_row * n_col + my_col

    def load(j):
        return pltpu.make_async_copy(
            phase_hbm.at[:, pl.ds(j * LANES, LANES)],
            ph.at[j, pl.ds(HALO, rows)],
            local_sem.at[j],
        )

    for j in range(blocks):
        load(j).start()
    load_mask = pltpu.make_async_copy(mask_hbm, mask_ref, local_sem.at[blocks])
    load_mask.start()

    barrier = pltpu.get_barrier_semaphore()

    def peer_of(d):
        peer = lax.rem(me + d, n_dev)
        return {"row": peer // n_col, "col": lax.rem(peer, n_col)}

    def far_first(act):
        for k in range(n_col):
            col = jnp.where(2 * my_col >= n_col, k, n_col - 1 - k)
            away = (col != my_col).astype(jnp.int32)

            def one(r, carry, col=col):
                act({"row": lax.rem(my_row + r, n_row), "col": col})
                return carry

            lax.fori_loop(1 - away, n_row, one, 0)

    def greet(peer):
        pl.semaphore_signal(barrier, inc=1, device_id=peer, device_id_type=MESH)

    far_first(greet)

    def exists(k):
        dr, dc = STEPS[k]
        ok = None
        for cond in (
            my_row > 0 if dr < 0 else (my_row < n_row - 1 if dr > 0 else None),
            my_col > 0 if dc < 0 else (my_col < n_col - 1 if dc > 0 else None),
        ):
            if cond is not None:
                ok = cond if ok is None else jnp.logical_and(ok, cond)
        return ok

    def landing(k):
        return in_side.at[k] if k < 4 else in_corner.at[k - 4]

    def source(k):
        if k < 4:
            return out_strip.at[k]
        dr, dc = STEPS[k]
        return out_strip.at[0 if dr < 0 else 1, :, pl.ds(0 if dc < 0 else cols - LANES, LANES)]

    for k in range(8):
        @pl.when(jnp.logical_not(exists(k)))
        def _(k=k):
            if k < 4:
                in_side[k] = jnp.zeros((2 * HALO, cols), jnp.float32)
            else:
                in_corner[k - 4] = jnp.zeros((2 * HALO, LANES), jnp.float32)

    load_mask.wait()
    tile_rows, tile_cols = rows // TILE, cols // TILE
    value = [
        [mask_ref[i, j].astype(jnp.float32) * diffusion for j in range(tile_cols)]
        for i in range(tile_rows)
    ]
    for j in range(tile_cols):
        cut = pl.ds(j * TILE, TILE)
        out_strip[0, HALO:, cut] = jnp.full((HALO, TILE), value[0][j], jnp.float32)
        out_strip[1, HALO:, cut] = jnp.full((HALO, TILE), value[-1][j], jnp.float32)
    for j in range(blocks):
        for i in range(tile_rows):
            a2[j, pl.ds(HALO + i * TILE, TILE), :] = jnp.full(
                (TILE, LANES), value[i][j * LANES // TILE], jnp.float32
            )
    for i in range(tile_rows):
        cut = pl.ds(i * TILE, TILE)
        out_strip[2, HALO:, cut] = jnp.full((HALO, TILE), value[i][0], jnp.float32)
        out_strip[3, HALO:, cut] = jnp.full((HALO, TILE), value[i][-1], jnp.float32)

    for j in range(blocks):
        load(j).wait()
    for j in range(blocks):
        cut = pl.ds(j * LANES, LANES)
        out_strip[0, :HALO, cut] = ph[j, pl.ds(HALO, HALO), :]
        out_strip[1, :HALO, cut] = ph[j, pl.ds(rows, HALO), :]
    out_strip[2, :HALO, :] = ph[0, pl.ds(HALO, rows), :].T[:HALO]
    out_strip[3, :HALO, :] = ph[blocks - 1, pl.ds(HALO, rows), :].T[LANES - HALO:]

    pl.semaphore_wait(barrier, n_dev - 1)

    def side_copy(k):
        dr, dc = STEPS[k]
        return pltpu.make_async_remote_copy(
            src_ref=source(k),
            dst_ref=landing(OPPOSITE[k]),
            send_sem=side_send.at[k],
            recv_sem=side_recv.at[OPPOSITE[k]],
            device_id={"row": my_row + dr, "col": my_col + dc},
            device_id_type=MESH,
        )

    def side_arrival(k):
        dr, dc = STEPS[k]
        return pltpu.make_async_remote_copy(
            src_ref=landing(k),
            dst_ref=landing(k),
            send_sem=side_send.at[k],
            recv_sem=side_recv.at[k],
            device_id={"row": my_row + dr, "col": my_col + dc},
            device_id_type=MESH,
        )

    for k in range(8):
        @pl.when(exists(k))
        def _(k=k):
            side_copy(k).start()
    for k in range(8):
        @pl.when(exists(k))
        def _(k=k):
            side_arrival(k).wait_recv()

    lane = lax.broadcasted_iota(jnp.int32, (HALO, LANES), 1)
    gap = jnp.zeros((LANES - 2 * HALO, rows), jnp.float32)
    for part, ref in ((slice(0, HALO), ph), (slice(HALO, 2 * HALO), a2)):
        for j in range(blocks):
            cut = pl.ds(j * LANES, LANES)
            ref[j, pl.ds(0, HALO), :] = in_side[0, part, cut]
            ref[j, pl.ds(HALO + rows, HALO), :] = in_side[1, part, cut]
        ref[blocks, pl.ds(HALO, rows), :] = jnp.concatenate(
            [in_side[3, part, :], gap, in_side[2, part, :]], axis=0
        ).T
        ref[blocks, pl.ds(0, HALO), :] = jnp.where(
            lane < LANES // 2, in_corner[1, part, :], in_corner[0, part, :]
        )
        ref[blocks, pl.ds(HALO + rows, HALO), :] = jnp.where(
            lane < LANES // 2, in_corner[3, part, :], in_corner[2, part, :]
        )

    def around(field, at, above, below, count, outer):
        column = lax.broadcasted_iota(jnp.int32, (count, LANES), 1)
        centre = [field[j, at, :] for j in range(blocks + 1)]
        ahead = [pltpu.roll(x, 1, 1) for x in centre]
        behind = [pltpu.roll(x, LANES - 1, 1) for x in centre]
        n = blocks + 1
        for j in range(n if outer else blocks):
            near = (
                field[j, above, :]
                + field[j, below, :]
                + jnp.where(column == 0, ahead[(j - 1) % n], ahead[j])
                + jnp.where(column == LANES - 1, behind[(j + 1) % n], behind[j])
            )
            yield j, centre[j], near

    def sweep(field, finish, n_sums, halo):
        if halo:
            for first in (1, tall - 1 - HALO):
                at, above, below = (pl.ds(first + shift, HALO) for shift in (0, -1, 1))
                for j, centre, near in around(field, at, above, below, HALO, True):
                    finish(j, centre, near, at)

        def step(i, sums):
            start = pl.multiple_of(i * CHUNK, 8)
            at = pl.ds(pl.multiple_of(start + HALO, 8), CHUNK)
            above = pl.ds(start + (HALO - 1), CHUNK)
            below = pl.ds(start + (HALO + 1), CHUNK)
            for j, centre, near in around(field, at, above, below, CHUNK, halo):
                terms = finish(j, centre, near, at)
                if j < blocks:
                    sums = tuple(s + t for s, t in zip(sums, terms))
            return sums

        zero = jnp.zeros((CHUNK, LANES), jnp.float32)
        return lax.fori_loop(0, rows // CHUNK, step, (zero,) * n_sums)

    def force_of(j, centre, near, at):
        act2 = a2[j, at, :]
        square = centre * centre
        act = act2 * (1.0 / diffusion)
        q[j, at, :] = act * (1.0 - 3.0 * square)
        u0[j, at, :] = act2 * (near - 4.0 * centre) + act * ((1.0 - square) * centre)
        return ()

    sweep(ph, force_of, 0, True)

    def power(dst, with_start):
        def finish(j, centre, near, at):
            image = a2[j, at, :] * near + q[j, at, :] * centre
            if dst is not None:
                dst[j, at, :] = image
            cross = centre * image
            if dst is None:
                return (cross,)
            if with_start:
                return (centre * centre, cross, image * image)
            return (cross, image * image)

        return finish

    def moments(b0, b1, b2, index):
        sums = sweep(b0, power(b1, True), 3, True)
        sums += sweep(b1, power(b2, False), 2, True)
        sums += sweep(b2, power(None, False), 1, False)
        lanes = lax.broadcasted_iota(jnp.int32, (1, LANES), 1)
        row = jnp.zeros((1, LANES), jnp.float32)
        for k, s in enumerate(sums):
            row = jnp.where(lanes == k, jnp.sum(s, keepdims=True), row)
        row_buf[index] = row
        gather[index, me] = row

        def send(peer):
            pltpu.make_async_remote_copy(
                src_ref=row_buf.at[index],
                dst_ref=gather.at[index, me],
                send_sem=red_send.at[index],
                recv_sem=red_recv.at[index],
                device_id=peer,
                device_id_type=MESH,
            ).start()

        far_first(send)
        others = gather.at[index, pl.ds(0, n_dev - 1)]
        done = pltpu.make_async_remote_copy(
            src_ref=others,
            dst_ref=others,
            send_sem=red_send.at[index],
            recv_sem=red_recv.at[index],
            device_id=peer_of(1),
            device_id_type=MESH,
        )
        done.wait_recv()
        total = jnp.sum(gather[index], axis=0)
        total = jnp.broadcast_to(total, (8, LANES))
        spot = lax.broadcasted_iota(jnp.int32, (8, LANES), 1)
        return [
            jnp.broadcast_to(
                jnp.sum(jnp.where(spot == k, total, 0.0), axis=1, keepdims=True), (8, LANES)
            )
            for k in range(MOMENTS)
        ]

    diag, lower, coefs = lanczos(moments(u0, u1, u2, 0))
    sub = lax.broadcasted_iota(jnp.int32, (8, LANES), 0)
    scale = jnp.where(sub < 4, 0.5, 1.0).astype(jnp.float32)
    mixed = to_powers(phi_weights(diag, lower, scale, 1), coefs)
    half = [0.5 * m[0:1, 0:1] for m in mixed]
    full = [m[4:5, 0:1] for m in mixed]

    def section_of(at, out_at):
        for j in range(blocks + 1):
            x0, x1, x2 = u0[j, at, :], u1[j, at, :], u2[j, at, :]
            here = ph[j, at, :]
            shift = half[0] * x0 + half[1] * x1 + half[2] * x2
            w0[j, at, :] = (a2[j, at, :] * (-1.0 / diffusion)) * shift * shift * (shift + 3.0 * here)
            if out_at is not None and j < blocks:
                sec[out_at, pl.ds(j * LANES, LANES)] = here + shift
                upd[out_at, pl.ds(j * LANES, LANES)] = here + full[0] * x0 + full[1] * x1 + full[2] * x2

    section_of(pl.ds(0, HALO), None)
    section_of(pl.ds(tall - HALO, HALO), None)

    def section_step(i, carry):
        start = pl.multiple_of(i * CHUNK, 8)
        section_of(pl.ds(pl.multiple_of(start + HALO, 8), CHUNK), pl.ds(start, CHUNK))
        return carry

    lax.fori_loop(0, rows // CHUNK, section_step, 0)

    diag, lower, coefs = lanczos(moments(w0, w1, w2, 1))
    third = [
        remainder_weight * m[0:1, 0:1]
        for m in to_powers(phi_weights(diag, lower, jnp.ones((8, LANES), jnp.float32), 3), coefs)
    ]

    for j in range(blocks):
        def final_step(i, carry, j=j):
            start = pl.multiple_of(i * FINAL, 8)
            at = pl.ds(pl.multiple_of(start + HALO, 8), FINAL)
            out_at = pl.ds(start, FINAL)
            cut = pl.ds(j * LANES, LANES)
            upd[out_at, cut] = upd[out_at, cut] + (
                third[0] * w0[j, at, :] + third[1] * w1[j, at, :] + third[2] * w2[j, at, :]
            )
            return carry

        lax.fori_loop(0, rows // FINAL, final_step, 0)
    for index in range(2):
        others = gather.at[index, pl.ds(0, n_dev - 1)]
        pltpu.make_async_remote_copy(
            src_ref=others, dst_ref=others, send_sem=red_send.at[index], recv_sem=red_recv.at[index],
            device_id=peer_of(1), device_id_type=MESH,
        ).wait_send()
    for k in range(8):
        @pl.when(exists(k))
        def _(k=k):
            side_copy(k).wait_send()


def body(n_row, n_col, phase, tile_mask):
    rows, cols = phase.shape
    n_dev = n_row * n_col
    blocks = cols // LANES
    block = pltpu.VMEM((blocks + 1, rows + 2 * HALO, LANES), jnp.float32)
    shape = jax.ShapeDtypeStruct((rows, cols), jnp.float32)
    vmem = pl.BlockSpec(memory_space=pltpu.VMEM)
    return pl.pallas_call(
        functools.partial(kernel, n_row, n_col),
        out_shape=(shape, shape),
        in_specs=[pl.BlockSpec(memory_space=pltpu.HBM), pl.BlockSpec(memory_space=pltpu.HBM)],
        out_specs=(vmem, vmem),
        scratch_shapes=[block] * 9 + [
            pltpu.SMEM(tile_mask.shape, jnp.int32),
            pltpu.VMEM((4, 2 * HALO, cols), jnp.float32),
            pltpu.VMEM((4, 2 * HALO, cols), jnp.float32),
            pltpu.VMEM((4, 2 * HALO, LANES), jnp.float32),
            pltpu.VMEM((2, 1, LANES), jnp.float32),
            pltpu.VMEM((2, n_dev, 1, LANES), jnp.float32),
            pltpu.SemaphoreType.DMA((blocks + 1,)),
            pltpu.SemaphoreType.DMA((8,)),
            pltpu.SemaphoreType.DMA((8,)),
            pltpu.SemaphoreType.DMA((2,)),
            pltpu.SemaphoreType.DMA((2,)),
        ],
        compiler_params=pltpu.CompilerParams(
            collective_id=0, has_side_effects=True, vmem_limit_bytes=24 << 20
        ),
        name="epirk_section",
    )(
        pltpu.with_memory_space_constraint(phase, pltpu.HBM),
        pltpu.with_memory_space_constraint(tile_mask, pltpu.HBM),
    )


def solution(mesh):
    spec = P("row", "col")
    run = functools.partial(body, mesh.shape["row"], mesh.shape["col"])
    return jax.shard_map(
        run, mesh=mesh, in_specs=(spec, spec), out_specs=(spec, spec), check_vma=False
    )
```

```python
import functools

import jax
import jax.numpy as jnp
from jax import lax
from jax.experimental import pallas as pl
from jax.experimental.pallas import tpu as pltpu
from jax.sharding import PartitionSpec as P

TILE = 256
HALO = 8
LANES = 128
CHUNK = 128
FINAL = 64
PIECES = 2
MOMENTS = 6
MESH = pl.DeviceIdType.MESH

diffusion = 2.0
remainder_weight = 32.0
offset = -4.0 * diffusion

STEPS = ((-1, 0), (1, 0), (0, -1), (0, 1), (-1, -1), (-1, 1), (1, -1), (1, 1))
OPPOSITE = (1, 0, 3, 2, 7, 6, 5, 4)


def phi_weights(diag, lower_sq, scale, order):
    s = scale * (1.0 / 1024.0)
    zero = jnp.zeros_like(s)
    one = jnp.ones_like(s)
    hess = [
        [diag[0] * s, lower_sq[0] * s, None],
        [s, diag[1] * s, lower_sq[1] * s],
        [None, s, diag[2] * s],
    ]
    eps = 1.0 / 1024.0
    term = [[one if i == j else zero for j in range(3)] for i in range(3)]
    total = [row[:] for row in term]
    side_term = [[zero] * order for _ in range(3)]
    side = [[zero] * order for _ in range(3)]
    tail = [1.0]
    for k in range(1, order):
        tail.append(tail[-1] * eps / k)
    for degree in range(1, 11):
        inv = 1.0 / degree
        new_term, new_side = [], []
        for i in range(3):
            row = []
            for j in range(3):
                acc = None
                for k in range(3):
                    if hess[k][j] is not None:
                        part = term[i][k] * hess[k][j]
                        acc = part if acc is None else acc + part
                row.append(acc * inv)
            new_term.append(row)
            new_side.append(
                [(term[i][0] if c == 0 else side_term[i][c - 1]) * (eps * inv) for c in range(order)]
            )
        term, side_term = new_term, new_side
        total = [[total[i][j] + term[i][j] for j in range(3)] for i in range(3)]
        side = [[side[i][c] + side_term[i][c] for c in range(order)] for i in range(3)]
    for _ in range(10):
        new_side = []
        for i in range(3):
            row = []
            for c in range(order):
                acc = side[i][c]
                for k in range(c):
                    acc = acc + side[i][k] * tail[c - k]
                for k in range(3):
                    acc = acc + total[i][k] * side[k][c]
                row.append(acc)
            new_side.append(row)
        total = [
            [
                total[i][0] * total[0][j] + total[i][1] * total[1][j] + total[i][2] * total[2][j]
                for j in range(3)
            ]
            for i in range(3)
        ]
        side = new_side
        tail = [sum(tail[k] * tail[c - k] for k in range(c + 1)) for c in range(order)]
    return [side[i][order - 1] for i in range(3)]


def lanczos(m):
    tiny = 1e-7
    a0 = m[1] / m[0]
    n1 = jnp.maximum(m[2] - a0 * m[1], tiny * m[2])
    h1 = n1 / m[0]
    a1 = (m[3] - 2.0 * a0 * m[2] + a0 * a0 * m[1]) / n1
    c1 = -(a0 + a1)
    c0 = a0 * a1 - h1
    n2 = jnp.maximum(m[4] + c1 * m[3] + c0 * m[2], tiny * m[4])
    h2 = n2 / n1
    a2 = (
        m[5] + 2.0 * c1 * m[4] + (c1 * c1 + 2.0 * c0) * m[3] + 2.0 * c0 * c1 * m[2] + c0 * c0 * m[1]
    ) / n2
    diag = [a0 + offset, a1 + offset, a2 + offset]
    return diag, [h1, h2], (a0, c1, c0)


def to_powers(y, coefs):
    a0, c1, c0 = coefs
    return (y[0] - a0 * y[1] + c0 * y[2], y[1] + c1 * y[2], y[2])


def kernel(
    n_row, n_col, phase_hbm, mask_hbm, upd, sec,
    ph, a2, q, u0, u1, u2, w0, w1, w2, mask_ref,
    out_strip, in_side, in_corner, row_buf, gather,
    local_sem, side_send, side_recv, red_send, red_recv,
):
    rows, cols = upd.shape
    blocks = cols // LANES
    tall = rows + 2 * HALO
    n_dev = n_row * n_col
    my_row = lax.axis_index("row")
    my_col = lax.axis_index("col")
    me = my_row * n_col + my_col

    def load(j):
        return pltpu.make_async_copy(
            phase_hbm.at[:, pl.ds(j * LANES, LANES)],
            ph.at[j, pl.ds(HALO, rows)],
            local_sem.at[j],
        )

    for j in range(blocks):
        load(j).start()
    load_mask = pltpu.make_async_copy(mask_hbm, mask_ref, local_sem.at[blocks])
    load_mask.start()

    barrier = pltpu.get_barrier_semaphore()

    def peer_of(d):
        peer = lax.rem(me + d, n_dev)
        return {"row": peer // n_col, "col": lax.rem(peer, n_col)}

    def far_first(act):
        for k in range(n_col):
            col = jnp.where(2 * my_col >= n_col, k, n_col - 1 - k)
            away = (col != my_col).astype(jnp.int32)

            def one(r, carry, col=col):
                act({"row": lax.rem(my_row + r, n_row), "col": col})
                return carry

            lax.fori_loop(1 - away, n_row, one, 0)

    def greet(peer):
        pl.semaphore_signal(barrier, inc=1, device_id=peer, device_id_type=MESH)

    far_first(greet)

    def exists(k):
        dr, dc = STEPS[k]
        ok = None
        for cond in (
            my_row > 0 if dr < 0 else (my_row < n_row - 1 if dr > 0 else None),
            my_col > 0 if dc < 0 else (my_col < n_col - 1 if dc > 0 else None),
        ):
            if cond is not None:
                ok = cond if ok is None else jnp.logical_and(ok, cond)
        return ok

    def landing(k):
        return in_side.at[k] if k < 4 else in_corner.at[k - 4]

    def source(k):
        if k < 4:
            return out_strip.at[k]
        dr, dc = STEPS[k]
        return out_strip.at[0 if dr < 0 else 1, :, pl.ds(0 if dc < 0 else cols - LANES, LANES)]

    for k in range(8):
        @pl.when(jnp.logical_not(exists(k)))
        def _(k=k):
            if k < 4:
                in_side[k] = jnp.zeros((2 * HALO, cols), jnp.float32)
            else:
                in_corner[k - 4] = jnp.zeros((2 * HALO, LANES), jnp.float32)

    load_mask.wait()
    tile_rows, tile_cols = rows // TILE, cols // TILE
    value = [
        [mask_ref[i, j].astype(jnp.float32) * diffusion for j in range(tile_cols)]
        for i in range(tile_rows)
    ]
    for j in range(tile_cols):
        cut = pl.ds(j * TILE, TILE)
        out_strip[0, HALO:, cut] = jnp.full((HALO, TILE), value[0][j], jnp.float32)
        out_strip[1, HALO:, cut] = jnp.full((HALO, TILE), value[-1][j], jnp.float32)
    for j in range(blocks):
        for i in range(tile_rows):
            a2[j, pl.ds(HALO + i * TILE, TILE), :] = jnp.full(
                (TILE, LANES), value[i][j * LANES // TILE], jnp.float32
            )
    for i in range(tile_rows):
        cut = pl.ds(i * TILE, TILE)
        out_strip[2, HALO:, cut] = jnp.full((HALO, TILE), value[i][0], jnp.float32)
        out_strip[3, HALO:, cut] = jnp.full((HALO, TILE), value[i][-1], jnp.float32)

    for j in range(blocks):
        load(j).wait()
    for j in range(blocks):
        cut = pl.ds(j * LANES, LANES)
        out_strip[0, :HALO, cut] = ph[j, pl.ds(HALO, HALO), :]
        out_strip[1, :HALO, cut] = ph[j, pl.ds(rows, HALO), :]
    out_strip[2, :HALO, :] = ph[0, pl.ds(HALO, rows), :].T[:HALO]
    out_strip[3, :HALO, :] = ph[blocks - 1, pl.ds(HALO, rows), :].T[LANES - HALO:]

    pl.semaphore_wait(barrier, n_dev - 1)

    def side_copy(k):
        dr, dc = STEPS[k]
        return pltpu.make_async_remote_copy(
            src_ref=source(k),
            dst_ref=landing(OPPOSITE[k]),
            send_sem=side_send.at[k],
            recv_sem=side_recv.at[OPPOSITE[k]],
            device_id={"row": my_row + dr, "col": my_col + dc},
            device_id_type=MESH,
        )

    def side_arrival(k):
        dr, dc = STEPS[k]
        return pltpu.make_async_remote_copy(
            src_ref=landing(k),
            dst_ref=landing(k),
            send_sem=side_send.at[k],
            recv_sem=side_recv.at[k],
            device_id={"row": my_row + dr, "col": my_col + dc},
            device_id_type=MESH,
        )

    for k in range(8):
        @pl.when(exists(k))
        def _(k=k):
            side_copy(k).start()
    for k in range(8):
        @pl.when(exists(k))
        def _(k=k):
            side_arrival(k).wait_recv()

    lane = lax.broadcasted_iota(jnp.int32, (HALO, LANES), 1)
    gap = jnp.zeros((LANES - 2 * HALO, rows), jnp.float32)
    for part, ref in ((slice(0, HALO), ph), (slice(HALO, 2 * HALO), a2)):
        for j in range(blocks):
            cut = pl.ds(j * LANES, LANES)
            ref[j, pl.ds(0, HALO), :] = in_side[0, part, cut]
            ref[j, pl.ds(HALO + rows, HALO), :] = in_side[1, part, cut]
        ref[blocks, pl.ds(HALO, rows), :] = jnp.concatenate(
            [in_side[3, part, :], gap, in_side[2, part, :]], axis=0
        ).T
        ref[blocks, pl.ds(0, HALO), :] = jnp.where(
            lane < LANES // 2, in_corner[1, part, :], in_corner[0, part, :]
        )
        ref[blocks, pl.ds(HALO + rows, HALO), :] = jnp.where(
            lane < LANES // 2, in_corner[3, part, :], in_corner[2, part, :]
        )

    def around(field, at, above, below, count, outer):
        column = lax.broadcasted_iota(jnp.int32, (count, LANES), 1)
        centre = [field[j, at, :] for j in range(blocks + 1)]
        ahead = [pltpu.roll(x, 1, 1) for x in centre]
        behind = [pltpu.roll(x, LANES - 1, 1) for x in centre]
        n = blocks + 1
        for j in range(n if outer else blocks):
            near = (
                field[j, above, :]
                + field[j, below, :]
                + jnp.where(column == 0, ahead[(j - 1) % n], ahead[j])
                + jnp.where(column == LANES - 1, behind[(j + 1) % n], behind[j])
            )
            yield j, centre[j], near

    def sweep(field, finish, n_sums, halo):
        if halo:
            for first in (1, tall - 1 - HALO):
                at, above, below = (pl.ds(first + shift, HALO) for shift in (0, -1, 1))
                for j, centre, near in around(field, at, above, below, HALO, True):
                    finish(j, centre, near, at)

        def step(i, sums):
            start = pl.multiple_of(i * CHUNK, 8)
            at = pl.ds(pl.multiple_of(start + HALO, 8), CHUNK)
            above = pl.ds(start + (HALO - 1), CHUNK)
            below = pl.ds(start + (HALO + 1), CHUNK)
            for j, centre, near in around(field, at, above, below, CHUNK, halo):
                terms = finish(j, centre, near, at)
                if j < blocks:
                    sums = tuple(s + t for s, t in zip(sums, terms))
            return sums

        zero = jnp.zeros((CHUNK, LANES), jnp.float32)
        return lax.fori_loop(0, rows // CHUNK, step, (zero,) * n_sums)

    def force_of(j, centre, near, at):
        act2 = a2[j, at, :]
        square = centre * centre
        act = act2 * (1.0 / diffusion)
        q[j, at, :] = act * (1.0 - 3.0 * square)
        u0[j, at, :] = act2 * (near - 4.0 * centre) + act * ((1.0 - square) * centre)
        return ()

    sweep(ph, force_of, 0, True)

    def power(dst, with_start):
        def finish(j, centre, near, at):
            image = a2[j, at, :] * near + q[j, at, :] * centre
            if dst is not None:
                dst[j, at, :] = image
            cross = centre * image
            if dst is None:
                return (cross,)
            if with_start:
                return (centre * centre, cross, image * image)
            return (cross, image * image)

        return finish

    def moments(b0, b1, b2, index, meanwhile):
        sums = sweep(b0, power(b1, True), 3, True)
        sums += sweep(b1, power(b2, False), 2, True)
        sums += sweep(b2, power(None, False), 1, False)
        lanes = lax.broadcasted_iota(jnp.int32, (1, LANES), 1)
        row = jnp.zeros((1, LANES), jnp.float32)
        for k, s in enumerate(sums):
            row = jnp.where(lanes == k, jnp.sum(s, keepdims=True), row)
        row_buf[index] = row
        gather[index, me] = row

        def send(peer):
            pltpu.make_async_remote_copy(
                src_ref=row_buf.at[index],
                dst_ref=gather.at[index, me],
                send_sem=red_send.at[index],
                recv_sem=red_recv.at[index],
                device_id=peer,
                device_id_type=MESH,
            ).start()

        far_first(send)
        meanwhile()
        others = gather.at[index, pl.ds(0, n_dev - 1)]
        done = pltpu.make_async_remote_copy(
            src_ref=others,
            dst_ref=others,
            send_sem=red_send.at[index],
            recv_sem=red_recv.at[index],
            device_id=peer_of(1),
            device_id_type=MESH,
        )
        done.wait_recv()
        total = jnp.sum(gather[index], axis=0)
        total = jnp.broadcast_to(total, (8, LANES))
        spot = lax.broadcasted_iota(jnp.int32, (8, LANES), 1)
        return [
            jnp.broadcast_to(
                jnp.sum(jnp.where(spot == k, total, 0.0), axis=1, keepdims=True), (8, LANES)
            )
            for k in range(MOMENTS)
        ]

    diag, lower, coefs = lanczos(moments(u0, u1, u2, 0, lambda: None))
    sub = lax.broadcasted_iota(jnp.int32, (8, LANES), 0)
    scale = jnp.where(sub < 4, 0.5, 1.0).astype(jnp.float32)
    mixed = to_powers(phi_weights(diag, lower, scale, 1), coefs)
    half = [0.5 * m[0:1, 0:1] for m in mixed]
    full = [m[4:5, 0:1] for m in mixed]

    def shift_of(j, at):
        return half[0] * u0[j, at, :] + half[1] * u1[j, at, :] + half[2] * u2[j, at, :]

    def remainder_of(at):
        for j in range(blocks + 1):
            shift = shift_of(j, at)
            weight = a2[j, at, :] * (-1.0 / diffusion)
            w0[j, at, :] = weight * shift * shift * (shift + 3.0 * ph[j, at, :])

    remainder_of(pl.ds(0, HALO))
    remainder_of(pl.ds(tall - HALO, HALO))

    def remainder_step(i, carry):
        remainder_of(pl.ds(pl.multiple_of(i * FINAL + HALO, 8), FINAL))
        return carry

    lax.fori_loop(0, rows // FINAL, remainder_step, 0)

    def results():
        def result_step(i, carry):
            start = pl.multiple_of(i * FINAL, 8)
            at = pl.ds(pl.multiple_of(start + HALO, 8), FINAL)
            out_at = pl.ds(start, FINAL)
            for j in range(blocks):
                cut = pl.ds(j * LANES, LANES)
                here = ph[j, at, :]
                sec[out_at, cut] = here + shift_of(j, at)
                upd[out_at, cut] = here + (
                    full[0] * u0[j, at, :] + full[1] * u1[j, at, :] + full[2] * u2[j, at, :]
                )
            return carry

        lax.fori_loop(0, rows // FINAL, result_step, 0)

    diag, lower, coefs = lanczos(moments(w0, w1, w2, 1, results))
    third = [
        remainder_weight * m[0:1, 0:1]
        for m in to_powers(phi_weights(diag, lower, jnp.ones((8, LANES), jnp.float32), 3), coefs)
    ]

    for j in range(blocks):
        def final_step(i, carry, j=j):
            start = pl.multiple_of(i * FINAL, 8)
            at = pl.ds(pl.multiple_of(start + HALO, 8), FINAL)
            out_at = pl.ds(start, FINAL)
            cut = pl.ds(j * LANES, LANES)
            upd[out_at, cut] = upd[out_at, cut] + (
                third[0] * w0[j, at, :] + third[1] * w1[j, at, :] + third[2] * w2[j, at, :]
            )
            return carry

        lax.fori_loop(0, rows // FINAL, final_step, 0)
    for index in range(2):
        others = gather.at[index, pl.ds(0, n_dev - 1)]
        pltpu.make_async_remote_copy(
            src_ref=others, dst_ref=others, send_sem=red_send.at[index], recv_sem=red_recv.at[index],
            device_id=peer_of(1), device_id_type=MESH,
        ).wait_send()
    for k in range(8):
        @pl.when(exists(k))
        def _(k=k):
            side_copy(k).wait_send()


def flush(upd, sec, upd_hbm, sec_hbm, sems):
    step = upd.shape[0] // PIECES
    copies = [
        pltpu.make_async_copy(
            src.at[pl.ds(i * step, step)], dst.at[pl.ds(i * step, step)], sems.at[k, i]
        )
        for i in range(PIECES)
        for k, (src, dst) in enumerate(((upd, upd_hbm), (sec, sec_hbm)))
    ]
    for copy in copies:
        copy.start()
    for copy in copies:
        copy.wait()


def body(n_row, n_col, phase, tile_mask):
    rows, cols = phase.shape
    n_dev = n_row * n_col
    blocks = cols // LANES
    block = pltpu.VMEM((blocks + 1, rows + 2 * HALO, LANES), jnp.float32)
    shape = jax.ShapeDtypeStruct((rows, cols), jnp.float32)
    vmem = pl.BlockSpec(memory_space=pltpu.VMEM)
    updated, section = pl.pallas_call(
        functools.partial(kernel, n_row, n_col),
        out_shape=(shape, shape),
        in_specs=[pl.BlockSpec(memory_space=pltpu.HBM), pl.BlockSpec(memory_space=pltpu.HBM)],
        out_specs=(vmem, vmem),
        scratch_shapes=[block] * 9 + [
            pltpu.SMEM(tile_mask.shape, jnp.int32),
            pltpu.VMEM((4, 2 * HALO, cols), jnp.float32),
            pltpu.VMEM((4, 2 * HALO, cols), jnp.float32),
            pltpu.VMEM((4, 2 * HALO, LANES), jnp.float32),
            pltpu.VMEM((2, 1, LANES), jnp.float32),
            pltpu.VMEM((2, n_dev, 1, LANES), jnp.float32),
            pltpu.SemaphoreType.DMA((blocks + 1,)),
            pltpu.SemaphoreType.DMA((8,)),
            pltpu.SemaphoreType.DMA((8,)),
            pltpu.SemaphoreType.DMA((2,)),
            pltpu.SemaphoreType.DMA((2,)),
        ],
        compiler_params=pltpu.CompilerParams(
            collective_id=0, has_side_effects=True, vmem_limit_bytes=24 << 20
        ),
        name="epirk_section",
    )(
        pltpu.with_memory_space_constraint(phase, pltpu.HBM),
        pltpu.with_memory_space_constraint(tile_mask, pltpu.HBM),
    )
    hbm = pl.BlockSpec(memory_space=pltpu.HBM)
    return pl.pallas_call(
        flush,
        out_shape=(shape, shape),
        in_specs=(vmem, vmem),
        out_specs=(hbm, hbm),
        scratch_shapes=[pltpu.SemaphoreType.DMA((2, PIECES))],
        compiler_params=pltpu.CompilerParams(vmem_limit_bytes=8 << 20),
        name="flush",
    )(updated, section)


def solution(mesh):
    spec = P("row", "col")
    run = functools.partial(body, mesh.shape["row"], mesh.shape["col"])
    return jax.shard_map(
        run, mesh=mesh, in_specs=(spec, spec), out_specs=(spec, spec), check_vma=False
    )
```

```python
import functools

import jax
import jax.numpy as jnp
from jax import lax
from jax.experimental import pallas as pl
from jax.experimental.pallas import tpu as pltpu
from jax.sharding import PartitionSpec as P

TILE = 256
HALO = 8
LANES = 128
CHUNK = 128
FINAL = 64
PIECES = 4
MOMENTS = 6
MESH = pl.DeviceIdType.MESH

diffusion = 2.0
remainder_weight = 32.0
offset = -4.0 * diffusion

STEPS = ((-1, 0), (1, 0), (0, -1), (0, 1), (-1, -1), (-1, 1), (1, -1), (1, 1))
OPPOSITE = (1, 0, 3, 2, 7, 6, 5, 4)


def phi_weights(diag, lower_sq, scale, order):
    s = scale * (1.0 / 1024.0)
    zero = jnp.zeros_like(s)
    one = jnp.ones_like(s)
    hess = [
        [diag[0] * s, lower_sq[0] * s, None],
        [s, diag[1] * s, lower_sq[1] * s],
        [None, s, diag[2] * s],
    ]
    eps = 1.0 / 1024.0
    term = [[one if i == j else zero for j in range(3)] for i in range(3)]
    total = [row[:] for row in term]
    side_term = [[zero] * order for _ in range(3)]
    side = [[zero] * order for _ in range(3)]
    tail = [1.0]
    for k in range(1, order):
        tail.append(tail[-1] * eps / k)
    for degree in range(1, 11):
        inv = 1.0 / degree
        new_term, new_side = [], []
        for i in range(3):
            row = []
            for j in range(3):
                acc = None
                for k in range(3):
                    if hess[k][j] is not None:
                        part = term[i][k] * hess[k][j]
                        acc = part if acc is None else acc + part
                row.append(acc * inv)
            new_term.append(row)
            new_side.append(
                [(term[i][0] if c == 0 else side_term[i][c - 1]) * (eps * inv) for c in range(order)]
            )
        term, side_term = new_term, new_side
        total = [[total[i][j] + term[i][j] for j in range(3)] for i in range(3)]
        side = [[side[i][c] + side_term[i][c] for c in range(order)] for i in range(3)]
    for _ in range(10):
        new_side = []
        for i in range(3):
            row = []
            for c in range(order):
                acc = side[i][c]
                for k in range(c):
                    acc = acc + side[i][k] * tail[c - k]
                for k in range(3):
                    acc = acc + total[i][k] * side[k][c]
                row.append(acc)
            new_side.append(row)
        total = [
            [
                total[i][0] * total[0][j] + total[i][1] * total[1][j] + total[i][2] * total[2][j]
                for j in range(3)
            ]
            for i in range(3)
        ]
        side = new_side
        tail = [sum(tail[k] * tail[c - k] for k in range(c + 1)) for c in range(order)]
    return [side[i][order - 1] for i in range(3)]


def lanczos(m):
    tiny = 1e-7
    a0 = m[1] / m[0]
    n1 = jnp.maximum(m[2] - a0 * m[1], tiny * m[2])
    h1 = n1 / m[0]
    a1 = (m[3] - 2.0 * a0 * m[2] + a0 * a0 * m[1]) / n1
    c1 = -(a0 + a1)
    c0 = a0 * a1 - h1
    n2 = jnp.maximum(m[4] + c1 * m[3] + c0 * m[2], tiny * m[4])
    h2 = n2 / n1
    a2 = (
        m[5] + 2.0 * c1 * m[4] + (c1 * c1 + 2.0 * c0) * m[3] + 2.0 * c0 * c1 * m[2] + c0 * c0 * m[1]
    ) / n2
    diag = [a0 + offset, a1 + offset, a2 + offset]
    return diag, [h1, h2], (a0, c1, c0)


def to_powers(y, coefs):
    a0, c1, c0 = coefs
    return (y[0] - a0 * y[1] + c0 * y[2], y[1] + c1 * y[2], y[2])


def kernel(
    n_row, n_col, phase_hbm, mask_hbm, upd, sec, w0, w1, w2, third,
    ph, a2, q, u0, u1, u2, mask_ref,
    out_strip, in_side, in_corner, row_buf, gather,
    local_sem, side_send, side_recv, red_send, red_recv,
):
    rows, cols = upd.shape
    blocks = cols // LANES
    tall = rows + 2 * HALO
    n_dev = n_row * n_col
    my_row = lax.axis_index("row")
    my_col = lax.axis_index("col")
    me = my_row * n_col + my_col

    def load(j):
        return pltpu.make_async_copy(
            phase_hbm.at[:, pl.ds(j * LANES, LANES)],
            ph.at[j, pl.ds(HALO, rows)],
            local_sem.at[j],
        )

    for j in range(blocks):
        load(j).start()
    load_mask = pltpu.make_async_copy(mask_hbm, mask_ref, local_sem.at[blocks])
    load_mask.start()

    barrier = pltpu.get_barrier_semaphore()

    def peer_of(d):
        peer = lax.rem(me + d, n_dev)
        return {"row": peer // n_col, "col": lax.rem(peer, n_col)}

    def far_first(act):
        for k in range(n_col):
            col = jnp.where(2 * my_col >= n_col, k, n_col - 1 - k)
            away = (col != my_col).astype(jnp.int32)

            def one(r, carry, col=col):
                act({"row": lax.rem(my_row + r, n_row), "col": col})
                return carry

            lax.fori_loop(1 - away, n_row, one, 0)

    def greet(peer):
        pl.semaphore_signal(barrier, inc=1, device_id=peer, device_id_type=MESH)

    far_first(greet)

    def exists(k):
        dr, dc = STEPS[k]
        ok = None
        for cond in (
            my_row > 0 if dr < 0 else (my_row < n_row - 1 if dr > 0 else None),
            my_col > 0 if dc < 0 else (my_col < n_col - 1 if dc > 0 else None),
        ):
            if cond is not None:
                ok = cond if ok is None else jnp.logical_and(ok, cond)
        return ok

    def landing(k):
        return in_side.at[k] if k < 4 else in_corner.at[k - 4]

    def source(k):
        if k < 4:
            return out_strip.at[k]
        dr, dc = STEPS[k]
        return out_strip.at[0 if dr < 0 else 1, :, pl.ds(0 if dc < 0 else cols - LANES, LANES)]

    for k in range(8):
        @pl.when(jnp.logical_not(exists(k)))
        def _(k=k):
            if k < 4:
                in_side[k] = jnp.zeros((2 * HALO, cols), jnp.float32)
            else:
                in_corner[k - 4] = jnp.zeros((2 * HALO, LANES), jnp.float32)

    load_mask.wait()
    tile_rows, tile_cols = rows // TILE, cols // TILE
    value = [
        [mask_ref[i, j].astype(jnp.float32) * diffusion for j in range(tile_cols)]
        for i in range(tile_rows)
    ]
    for j in range(tile_cols):
        cut = pl.ds(j * TILE, TILE)
        out_strip[0, HALO:, cut] = jnp.full((HALO, TILE), value[0][j], jnp.float32)
        out_strip[1, HALO:, cut] = jnp.full((HALO, TILE), value[-1][j], jnp.float32)
    for j in range(blocks):
        for i in range(tile_rows):
            a2[j, pl.ds(HALO + i * TILE, TILE), :] = jnp.full(
                (TILE, LANES), value[i][j * LANES // TILE], jnp.float32
            )
    for i in range(tile_rows):
        cut = pl.ds(i * TILE, TILE)
        out_strip[2, HALO:, cut] = jnp.full((HALO, TILE), value[i][0], jnp.float32)
        out_strip[3, HALO:, cut] = jnp.full((HALO, TILE), value[i][-1], jnp.float32)

    for j in range(blocks):
        load(j).wait()
    for j in range(blocks):
        cut = pl.ds(j * LANES, LANES)
        out_strip[0, :HALO, cut] = ph[j, pl.ds(HALO, HALO), :]
        out_strip[1, :HALO, cut] = ph[j, pl.ds(rows, HALO), :]
    out_strip[2, :HALO, :] = ph[0, pl.ds(HALO, rows), :].T[:HALO]
    out_strip[3, :HALO, :] = ph[blocks - 1, pl.ds(HALO, rows), :].T[LANES - HALO:]

    pl.semaphore_wait(barrier, n_dev - 1)

    def side_copy(k):
        dr, dc = STEPS[k]
        return pltpu.make_async_remote_copy(
            src_ref=source(k),
            dst_ref=landing(OPPOSITE[k]),
            send_sem=side_send.at[k],
            recv_sem=side_recv.at[OPPOSITE[k]],
            device_id={"row": my_row + dr, "col": my_col + dc},
            device_id_type=MESH,
        )

    def side_arrival(k):
        dr, dc = STEPS[k]
        return pltpu.make_async_remote_copy(
            src_ref=landing(k),
            dst_ref=landing(k),
            send_sem=side_send.at[k],
            recv_sem=side_recv.at[k],
            device_id={"row": my_row + dr, "col": my_col + dc},
            device_id_type=MESH,
        )

    for k in range(8):
        @pl.when(exists(k))
        def _(k=k):
            side_copy(k).start()
    for k in range(8):
        @pl.when(exists(k))
        def _(k=k):
            side_arrival(k).wait_recv()

    lane = lax.broadcasted_iota(jnp.int32, (HALO, LANES), 1)
    gap = jnp.zeros((LANES - 2 * HALO, rows), jnp.float32)
    for part, ref in ((slice(0, HALO), ph), (slice(HALO, 2 * HALO), a2)):
        for j in range(blocks):
            cut = pl.ds(j * LANES, LANES)
            ref[j, pl.ds(0, HALO), :] = in_side[0, part, cut]
            ref[j, pl.ds(HALO + rows, HALO), :] = in_side[1, part, cut]
        ref[blocks, pl.ds(HALO, rows), :] = jnp.concatenate(
            [in_side[3, part, :], gap, in_side[2, part, :]], axis=0
        ).T
        ref[blocks, pl.ds(0, HALO), :] = jnp.where(
            lane < LANES // 2, in_corner[1, part, :], in_corner[0, part, :]
        )
        ref[blocks, pl.ds(HALO + rows, HALO), :] = jnp.where(
            lane < LANES // 2, in_corner[3, part, :], in_corner[2, part, :]
        )

    def around(field, at, above, below, count, outer):
        column = lax.broadcasted_iota(jnp.int32, (count, LANES), 1)
        centre = [field[j, at, :] for j in range(blocks + 1)]
        ahead = [pltpu.roll(x, 1, 1) for x in centre]
        behind = [pltpu.roll(x, LANES - 1, 1) for x in centre]
        n = blocks + 1
        for j in range(n if outer else blocks):
            near = (
                field[j, above, :]
                + field[j, below, :]
                + jnp.where(column == 0, ahead[(j - 1) % n], ahead[j])
                + jnp.where(column == LANES - 1, behind[(j + 1) % n], behind[j])
            )
            yield j, centre[j], near

    def sweep(field, finish, n_sums, halo):
        if halo:
            for first in (1, tall - 1 - HALO):
                at, above, below = (pl.ds(first + shift, HALO) for shift in (0, -1, 1))
                for j, centre, near in around(field, at, above, below, HALO, True):
                    finish(j, centre, near, at)

        def step(i, sums):
            start = pl.multiple_of(i * CHUNK, 8)
            at = pl.ds(pl.multiple_of(start + HALO, 8), CHUNK)
            above = pl.ds(start + (HALO - 1), CHUNK)
            below = pl.ds(start + (HALO + 1), CHUNK)
            for j, centre, near in around(field, at, above, below, CHUNK, halo):
                terms = finish(j, centre, near, at)
                if j < blocks:
                    sums = tuple(s + t for s, t in zip(sums, terms))
            return sums

        zero = jnp.zeros((CHUNK, LANES), jnp.float32)
        return lax.fori_loop(0, rows // CHUNK, step, (zero,) * n_sums)

    def force_of(j, centre, near, at):
        act2 = a2[j, at, :]
        square = centre * centre
        act = act2 * (1.0 / diffusion)
        q[j, at, :] = act * (1.0 - 3.0 * square)
        u0[j, at, :] = act2 * (near - 4.0 * centre) + act * ((1.0 - square) * centre)
        return ()

    sweep(ph, force_of, 0, True)

    def power(dst, with_start):
        def finish(j, centre, near, at):
            image = a2[j, at, :] * near + q[j, at, :] * centre
            if dst is not None:
                dst[j, at, :] = image
            cross = centre * image
            if dst is None:
                return (cross,)
            if with_start:
                return (centre * centre, cross, image * image)
            return (cross, image * image)

        return finish

    def moments(b0, b1, b2, index, meanwhile):
        sums = sweep(b0, power(b1, True), 3, True)
        sums += sweep(b1, power(b2, False), 2, True)
        sums += sweep(b2, power(None, False), 1, False)
        lanes = lax.broadcasted_iota(jnp.int32, (1, LANES), 1)
        row = jnp.zeros((1, LANES), jnp.float32)
        for k, s in enumerate(sums):
            row = jnp.where(lanes == k, jnp.sum(s, keepdims=True), row)
        row_buf[index] = row
        gather[index, me] = row

        def send(peer):
            pltpu.make_async_remote_copy(
                src_ref=row_buf.at[index],
                dst_ref=gather.at[index, me],
                send_sem=red_send.at[index],
                recv_sem=red_recv.at[index],
                device_id=peer,
                device_id_type=MESH,
            ).start()

        far_first(send)
        meanwhile()
        others = gather.at[index, pl.ds(0, n_dev - 1)]
        done = pltpu.make_async_remote_copy(
            src_ref=others,
            dst_ref=others,
            send_sem=red_send.at[index],
            recv_sem=red_recv.at[index],
            device_id=peer_of(1),
            device_id_type=MESH,
        )
        done.wait_recv()
        total = jnp.sum(gather[index], axis=0)
        total = jnp.broadcast_to(total, (8, LANES))
        spot = lax.broadcasted_iota(jnp.int32, (8, LANES), 1)
        return [
            jnp.broadcast_to(
                jnp.sum(jnp.where(spot == k, total, 0.0), axis=1, keepdims=True), (8, LANES)
            )
            for k in range(MOMENTS)
        ]

    diag, lower, coefs = lanczos(moments(u0, u1, u2, 0, lambda: None))
    sub = lax.broadcasted_iota(jnp.int32, (8, LANES), 0)
    scale = jnp.where(sub < 4, 0.5, 1.0).astype(jnp.float32)
    mixed = to_powers(phi_weights(diag, lower, scale, 1), coefs)
    half = [0.5 * m[0:1, 0:1] for m in mixed]
    full = [m[4:5, 0:1] for m in mixed]

    def shift_of(j, at):
        return half[0] * u0[j, at, :] + half[1] * u1[j, at, :] + half[2] * u2[j, at, :]

    def remainder_of(at):
        for j in range(blocks + 1):
            shift = shift_of(j, at)
            weight = a2[j, at, :] * (-1.0 / diffusion)
            w0[j, at, :] = weight * shift * shift * (shift + 3.0 * ph[j, at, :])

    remainder_of(pl.ds(0, HALO))
    remainder_of(pl.ds(tall - HALO, HALO))

    def remainder_step(i, carry):
        remainder_of(pl.ds(pl.multiple_of(i * FINAL + HALO, 8), FINAL))
        return carry

    lax.fori_loop(0, rows // FINAL, remainder_step, 0)

    def results():
        def result_step(i, carry):
            start = pl.multiple_of(i * FINAL, 8)
            at = pl.ds(pl.multiple_of(start + HALO, 8), FINAL)
            out_at = pl.ds(start, FINAL)
            for j in range(blocks):
                cut = pl.ds(j * LANES, LANES)
                here = ph[j, at, :]
                sec[out_at, cut] = here + shift_of(j, at)
                upd[out_at, cut] = here + (
                    full[0] * u0[j, at, :] + full[1] * u1[j, at, :] + full[2] * u2[j, at, :]
                )
            return carry

        lax.fori_loop(0, rows // FINAL, result_step, 0)

    diag, lower, coefs = lanczos(moments(w0, w1, w2, 1, results))
    weights = phi_weights(diag, lower, jnp.ones((8, LANES), jnp.float32), 3)
    for k, m in enumerate(to_powers(weights, coefs)):
        third[k] = remainder_weight * m
    for index in range(2):
        others = gather.at[index, pl.ds(0, n_dev - 1)]
        pltpu.make_async_remote_copy(
            src_ref=others, dst_ref=others, send_sem=red_send.at[index], recv_sem=red_recv.at[index],
            device_id=peer_of(1), device_id_type=MESH,
        ).wait_send()
    for k in range(8):
        @pl.when(exists(k))
        def _(k=k):
            side_copy(k).wait_send()


def flush(upd, sec, w0, w1, w2, third, upd_hbm, sec_hbm, total, sems):
    rows, cols = upd.shape
    step = rows // PIECES

    def copy(k, i):
        src, dst = ((total, upd_hbm), (sec, sec_hbm))[k]
        at = pl.ds(i * step, step)
        return pltpu.make_async_copy(src.at[at], dst.at[at], sems.at[k, i])

    for i in range(PIECES):
        copy(1, i).start()
    weight = [third[k, 0:1, :] for k in range(3)]
    for i in range(PIECES):
        def part(p, carry, i=i):
            start = pl.multiple_of(i * step + p * FINAL, 8)
            at = pl.ds(start, FINAL)
            inner = pl.ds(pl.multiple_of(start + HALO, 8), FINAL)
            for j in range(cols // LANES):
                cut = pl.ds(j * LANES, LANES)
                total[at, cut] = upd[at, cut] + (
                    weight[0] * w0[j, inner, :]
                    + weight[1] * w1[j, inner, :]
                    + weight[2] * w2[j, inner, :]
                )
            return carry

        lax.fori_loop(0, step // FINAL, part, 0)
        copy(0, i).start()
    for k in range(2):
        for i in range(PIECES):
            copy(k, i).wait()


def body(n_row, n_col, phase, tile_mask):
    rows, cols = phase.shape
    n_dev = n_row * n_col
    blocks = cols // LANES
    block = pltpu.VMEM((blocks + 1, rows + 2 * HALO, LANES), jnp.float32)
    shape = jax.ShapeDtypeStruct((rows, cols), jnp.float32)
    vmem = pl.BlockSpec(memory_space=pltpu.VMEM)
    field = jax.ShapeDtypeStruct((blocks + 1, rows + 2 * HALO, LANES), jnp.float32)
    small = jax.ShapeDtypeStruct((3, 8, LANES), jnp.float32)
    parts = pl.pallas_call(
        functools.partial(kernel, n_row, n_col),
        out_shape=(shape, shape, field, field, field, small),
        in_specs=[pl.BlockSpec(memory_space=pltpu.HBM), pl.BlockSpec(memory_space=pltpu.HBM)],
        out_specs=(vmem,) * 6,
        scratch_shapes=[block] * 6 + [
            pltpu.SMEM(tile_mask.shape, jnp.int32),
            pltpu.VMEM((4, 2 * HALO, cols), jnp.float32),
            pltpu.VMEM((4, 2 * HALO, cols), jnp.float32),
            pltpu.VMEM((4, 2 * HALO, LANES), jnp.float32),
            pltpu.VMEM((2, 1, LANES), jnp.float32),
            pltpu.VMEM((2, n_dev, 1, LANES), jnp.float32),
            pltpu.SemaphoreType.DMA((blocks + 1,)),
            pltpu.SemaphoreType.DMA((8,)),
            pltpu.SemaphoreType.DMA((8,)),
            pltpu.SemaphoreType.DMA((2,)),
            pltpu.SemaphoreType.DMA((2,)),
        ],
        compiler_params=pltpu.CompilerParams(
            collective_id=0, has_side_effects=True, vmem_limit_bytes=24 << 20
        ),
        name="epirk_section",
    )(
        pltpu.with_memory_space_constraint(phase, pltpu.HBM),
        pltpu.with_memory_space_constraint(tile_mask, pltpu.HBM),
    )
    hbm = pl.BlockSpec(memory_space=pltpu.HBM)
    return pl.pallas_call(
        flush,
        out_shape=(shape, shape),
        in_specs=(vmem,) * 6,
        out_specs=(hbm, hbm),
        scratch_shapes=[
            pltpu.VMEM((rows, cols), jnp.float32), pltpu.SemaphoreType.DMA((2, PIECES))
        ],
        compiler_params=pltpu.CompilerParams(vmem_limit_bytes=16 << 20),
        name="flush",
    )(*parts)


def solution(mesh):
    spec = P("row", "col")
    run = functools.partial(body, mesh.shape["row"], mesh.shape["col"])
    return jax.shard_map(
        run, mesh=mesh, in_specs=(spec, spec), out_specs=(spec, spec), check_vma=False
    )
```
